32 devices in a mesh: seq: 4 (over y, x), dp: 8 (over z, core).
Axes of the slice: x: 2, y: 2, z: 4, core: 2. Of those that a mesh axis runs over, the one named last changes fastest.
Arguments:
- layer_input: bfloat16 [8, 1024, 8192], P('dp', 'seq'), may hold values from -400 to 400
- frozen_queries: bfloat16 [8, 1024, 6144], P('dp', 'seq'), may hold values from -70 to 70
- frozen_keys: bfloat16 [8, 1024, 768], P('dp', 'seq'), may hold values from -6 to 6
- frozen_values: bfloat16 [8, 1024, 768], P('dp', 'seq'), may hold values from -6 to 6
- output_gradient: bfloat16 [8, 1024, 6144], P('dp', 'seq'), may hold values from -6 to 6
- norm_scale_vector: bfloat16 [8192], replicated, may hold values from 0.5 to 1.5
- query_down_weight: bfloat16 [8, 8192], replicated, may hold values from -0.0625 to 0.0625
- query_up_weight: bfloat16 [8, 6144], replicated, may hold values from -2 to 2
- value_down_weight: bfloat16 [8, 8192], replicated, may hold values from -0.0625 to 0.0625
- value_up_weight: bfloat16 [8, 768], replicated, may hold values from -2 to 2
- head_ordering: int32 [6], replicated, may hold values from 0 to 5, each once
Outputs:
- grad_query_a: float32 [8, 8192], replicated
- grad_query_b: float32 [8, 6144], replicated
- grad_value_a: float32 [8, 8192], replicated
- grad_value_b: float32 [8, 768], replicated
- grad_gain: float32 [8192], replicated
The draws below stay inside these ranges and needn't reach their ends.
Inputs may be any that keep to these rules, and one draw needn't show every extreme that they name: `head_ordering`: a permutation of the 6 key-value heads.
All inputs are finite; a program needn't handle non-finite values.
Results may differ from the reference program's by a relative error of at most 0.012.
The reference program's roundings to bfloat16 on the way count: a program that leaves them out, or rounds other values in their place, can miss the bound.
Values may be sent and summed in bfloat16 or wider, within the bound.
A program may use at most 128 MiB of HBM per device.

```python
import math
from functools import partial
import jax
import jax.numpy as jnp
from jax import lax

MODEL_WIDTH = 8192
HEAD_SIZE = 128
QUERY_HEADS = 48
KEY_VALUE_HEADS = 6
ADAPTER_RANK = 8
G = 512
SEQUENCE_LENGTH = 1024
BATCH_COUNT = 8


def drawn_pair(key):
    query_layout = (BATCH_COUNT, SEQUENCE_LENGTH, KEY_VALUE_HEADS, QUERY_HEADS // KEY_VALUE_HEADS, HEAD_SIZE)
    key_layout = (BATCH_COUNT, SEQUENCE_LENGTH, KEY_VALUE_HEADS, HEAD_SIZE)
    key_rows = jax.random.truncated_normal(jax.random.fold_in(key, 102), -6.0, 6.0, key_layout, jnp.float32)
    queries = jax.random.truncated_normal(jax.random.fold_in(key, 103), -6.0, 6.0, query_layout, jnp.float32)
    return (queries, key_rows)


def draw_frozen_queries(key, part):
    queries, key_rows = drawn_pair(key)
    return queries.reshape(BATCH_COUNT, SEQUENCE_LENGTH, QUERY_HEADS * HEAD_SIZE).astype(jnp.bfloat16)


def draw_frozen_keys(key, part):
    queries, key_rows = drawn_pair(key)
    return key_rows.reshape(BATCH_COUNT, SEQUENCE_LENGTH, KEY_VALUE_HEADS * HEAD_SIZE).astype(jnp.bfloat16)


def draw_layer_input(key, part):
    row_scale = jnp.exp(jax.random.uniform(jax.random.fold_in(key, 201), (BATCH_COUNT, SEQUENCE_LENGTH, 1), jnp.float32, 0.0, math.log(10.0)))
    col_scale = jnp.exp(jax.random.uniform(jax.random.fold_in(key, 202), (1, 1, MODEL_WIDTH), jnp.float32, 0.0, math.log(10.0)))
    base = jax.random.truncated_normal(jax.random.fold_in(key, 203), -4.0, 4.0, (BATCH_COUNT, SEQUENCE_LENGTH, MODEL_WIDTH), jnp.float32)
    return (base * row_scale * col_scale).astype(jnp.bfloat16)


def block_scale(key, shape, shards, low, high):
    factor_of = 1.0
    for dim, shards_of in shards:
        heights = jax.random.uniform(jax.random.fold_in(jax.random.fold_in(key, 6), dim), (shards_of,), jnp.float32, low / len(shards), high / len(shards))
        factor_of = factor_of * jnp.repeat(jnp.exp(heights), shape[dim] // shards_of).reshape((-1,) + (1,) * (len(shape) - 1 - dim))
    return factor_of


def normal_values(stream_key, shape, deviation, reach, cuts=(), kind=jnp.bfloat16):
    loudness = block_scale(stream_key, shape, cuts, -0.22, 0.18) if cuts else 1.0
    values = jax.random.normal(stream_key, shape, jnp.float32) * deviation * loudness
    return jnp.minimum(jnp.maximum(values, -reach), reach).astype(kind)


def setup_inputs(seed: int = 0) -> dict:
    arg_keys = jax.random.split(jax.random.key(seed), 12)
    layer_input = draw_layer_input(jax.random.fold_in(arg_keys[11], 71), 0)
    frozen_queries = draw_frozen_queries(jax.random.fold_in(arg_keys[11], 71), 0)
    frozen_keys = draw_frozen_keys(jax.random.fold_in(arg_keys[11], 71), 0)
    frozen_values = normal_values(arg_keys[3], (BATCH_COUNT, SEQUENCE_LENGTH, KEY_VALUE_HEADS * HEAD_SIZE), 1.0, 6.0, ((0, 8), (1, 4)))
    output_gradient = normal_values(arg_keys[4], (BATCH_COUNT, SEQUENCE_LENGTH, QUERY_HEADS * HEAD_SIZE), 1.0, 6.0, ((0, 8), (1, 4)))
    norm_scale_vector = jnp.clip(jax.random.uniform(arg_keys[5], (MODEL_WIDTH,), jnp.float32, 0.5, 1.5), 0.5, 1.5).astype(jnp.bfloat16)
    query_down_weight = normal_values(arg_keys[6], (ADAPTER_RANK, MODEL_WIDTH), MODEL_WIDTH ** -0.5, 0.0625)
    query_up_weight = normal_values(arg_keys[7], (ADAPTER_RANK, QUERY_HEADS * HEAD_SIZE), ADAPTER_RANK ** -0.5, 2.0)
    value_down_weight = normal_values(arg_keys[8], (ADAPTER_RANK, MODEL_WIDTH), MODEL_WIDTH ** -0.5, 0.0625)
    value_up_weight = normal_values(arg_keys[9], (ADAPTER_RANK, KEY_VALUE_HEADS * HEAD_SIZE), ADAPTER_RANK ** -0.5, 2.0)
    head_ordering = jax.random.permutation(arg_keys[10], KEY_VALUE_HEADS).astype(jnp.int32)
    return dict(layer_input=layer_input, frozen_queries=frozen_queries, frozen_keys=frozen_keys, frozen_values=frozen_values, output_gradient=output_gradient, norm_scale_vector=norm_scale_vector, query_down_weight=query_down_weight, query_up_weight=query_up_weight, value_down_weight=value_down_weight, value_up_weight=value_up_weight, head_ordering=head_ordering)


EPS = 1e-05
ADAPTER_SCALE = 2.0

def attend_group(query_rows, key_rows, values, grad_out, allowed):
    factor = 1.0 / math.sqrt(HEAD_SIZE)
    keys_f = key_rows.astype(jnp.float32)
    values_f = values.astype(jnp.float32)
    grads_f = grad_out.astype(jnp.float32)
    scores = jnp.einsum('tgd,ud->gtu', query_rows.astype(jnp.float32), keys_f) * factor
    scores = jnp.where(allowed[None], scores, -jnp.inf)
    row_max = lax.optimization_barrier(jnp.max(scores, axis=-1, keepdims=True))
    exponent = jnp.exp(scores - row_max)
    probs_full = exponent / lax.optimization_barrier(jnp.sum(exponent, axis=-1, keepdims=True))
    weights = lax.optimization_barrier(probs_full.astype(jnp.bfloat16)).astype(jnp.float32)
    attended = jnp.einsum('gtu,ud->tgd', weights, values_f)
    delta = lax.optimization_barrier(jnp.sum(grads_f * attended, axis=-1))
    dprob = jnp.einsum('tgd,ud->gtu', grads_f, values_f)
    dscore = probs_full * (dprob - delta.T[:, :, None])
    dscore_b = lax.optimization_barrier(dscore.astype(jnp.bfloat16)).astype(jnp.float32)
    query_gradient = jnp.einsum('gtu,ud->tgd', dscore_b, keys_f) * factor
    value_gradient = jnp.einsum('gtu,tgd->ud', weights, grads_f)
    return (query_gradient, value_gradient)

def head_grads(operands):
    query_h, keys_h, values_h, grads_h, offset = operands

    def regroup(array):
        rolled_array = jnp.roll(array, -offset, axis=0)
        return rolled_array.reshape((SEQUENCE_LENGTH // G, G) + array.shape[1:])
    positions = jnp.arange(G)
    causal = positions[None, :] <= positions[:, None]
    query_gradient, value_gradient = jax.vmap(partial(attend_group, allowed=causal))(regroup(query_h), regroup(keys_h), regroup(values_h), regroup(grads_h))
    query_gradient = jnp.roll(query_gradient.reshape(query_h.shape), offset, axis=0)
    value_gradient = jnp.roll(value_gradient.reshape(keys_h.shape), offset, axis=0)
    return (query_gradient.astype(jnp.bfloat16), value_gradient.astype(jnp.bfloat16))

def reference(layer_input, frozen_queries, frozen_keys, frozen_values, output_gradient, norm_scale_vector, query_down_weight, query_up_weight, value_down_weight, value_up_weight, head_ordering):
    displaced_index = head_ordering[:KEY_VALUE_HEADS // 2]
    displaced_mask = jnp.any(displaced_index[:, None] == jnp.arange(KEY_VALUE_HEADS, dtype=jnp.int32)[None, :], axis=0)
    shift_amounts = jnp.where(displaced_mask, G // 2, 0).astype(jnp.int32)

    def one_sequence(totals, operands):
        hidden_s, query_slices, key_slices, value_slices, gradient_slices = operands
        hidden_f = hidden_s.astype(jnp.float32)
        inverse = lax.rsqrt(lax.optimization_barrier(jnp.mean(hidden_f * hidden_f, axis=-1, keepdims=True)) + EPS)
        unit = hidden_f * inverse
        normalized_input = (unit * norm_scale_vector.astype(jnp.float32)).astype(jnp.bfloat16)
        query_inner = jnp.dot(normalized_input, query_down_weight.T, preferred_element_type=jnp.float32).astype(jnp.bfloat16)
        value_inner = jnp.dot(normalized_input, value_down_weight.T, preferred_element_type=jnp.float32).astype(jnp.bfloat16)
        query_rows = (query_slices.astype(jnp.float32) + ADAPTER_SCALE * jnp.dot(query_inner, query_up_weight, preferred_element_type=jnp.float32)).astype(jnp.bfloat16)
        value_rows = (value_slices.astype(jnp.float32) + ADAPTER_SCALE * jnp.dot(value_inner, value_up_weight, preferred_element_type=jnp.float32)).astype(jnp.bfloat16)
        head_wise = (jnp.moveaxis(query_rows.reshape(SEQUENCE_LENGTH, KEY_VALUE_HEADS, QUERY_HEADS // KEY_VALUE_HEADS, HEAD_SIZE), 1, 0), jnp.moveaxis(key_slices.reshape(SEQUENCE_LENGTH, KEY_VALUE_HEADS, HEAD_SIZE), 1, 0), jnp.moveaxis(value_rows.reshape(SEQUENCE_LENGTH, KEY_VALUE_HEADS, HEAD_SIZE), 1, 0), jnp.moveaxis(gradient_slices.reshape(SEQUENCE_LENGTH, KEY_VALUE_HEADS, QUERY_HEADS // KEY_VALUE_HEADS, HEAD_SIZE), 1, 0), shift_amounts)
        query_gradient, value_gradient = lax.map(head_grads, head_wise)
        query_gradient = jnp.moveaxis(query_gradient, 0, 1).reshape(SEQUENCE_LENGTH, QUERY_HEADS * HEAD_SIZE)
        value_gradient = jnp.moveaxis(value_gradient, 0, 1).reshape(SEQUENCE_LENGTH, KEY_VALUE_HEADS * HEAD_SIZE)
        query_up_unscaled = ADAPTER_SCALE * jnp.dot(query_inner.T, query_gradient, preferred_element_type=jnp.float32)
        value_up_unscaled = ADAPTER_SCALE * jnp.dot(value_inner.T, value_gradient, preferred_element_type=jnp.float32)
        query_gradient_inner = (ADAPTER_SCALE * jnp.dot(query_gradient, query_up_weight.T, preferred_element_type=jnp.float32)).astype(jnp.bfloat16)
        value_gradient_inner = (ADAPTER_SCALE * jnp.dot(value_gradient, value_up_weight.T, preferred_element_type=jnp.float32)).astype(jnp.bfloat16)
        raw_qa = jnp.dot(query_gradient_inner.T, normalized_input, preferred_element_type=jnp.float32)
        raw_va = jnp.dot(value_gradient_inner.T, normalized_input, preferred_element_type=jnp.float32)
        normalized_gradient = jnp.dot(query_gradient_inner, query_down_weight, preferred_element_type=jnp.float32) + jnp.dot(value_gradient_inner, value_down_weight, preferred_element_type=jnp.float32)
        raw_gain = lax.optimization_barrier(jnp.sum(normalized_gradient * unit, axis=0))
        fresh = (raw_qa, query_up_unscaled, raw_va, value_up_unscaled, raw_gain)
        return (tuple((total + term for total, term in zip(totals, fresh))), None)
    start_position = (jnp.zeros((ADAPTER_RANK, MODEL_WIDTH), jnp.float32), jnp.zeros((ADAPTER_RANK, QUERY_HEADS * HEAD_SIZE), jnp.float32), jnp.zeros((ADAPTER_RANK, MODEL_WIDTH), jnp.float32), jnp.zeros((ADAPTER_RANK, KEY_VALUE_HEADS * HEAD_SIZE), jnp.float32), jnp.zeros((MODEL_WIDTH,), jnp.float32))
    totals, unused = lax.scan(one_sequence, start_position, (layer_input, frozen_queries, frozen_keys, frozen_values, output_gradient))
    squares = jnp.zeros((), jnp.float32)
    for part in totals:
        squares = squares + jnp.sum(part * part)
    listed_items = ADAPTER_RANK * (2 * MODEL_WIDTH + QUERY_HEADS * HEAD_SIZE + KEY_VALUE_HEADS * HEAD_SIZE) + MODEL_WIDTH
    factor = jnp.minimum(1.0, math.sqrt(listed_items) / jnp.sqrt(squares))
    return (totals[0] * factor, totals[1] * factor, totals[2] * factor, totals[3] * factor, totals[4] * factor)
```

```python
import functools
import math

import jax
import jax.numpy as jnp
from jax import lax
from jax.experimental import pallas as pl
from jax.experimental.pallas import tpu as pltpu
from jax.sharding import PartitionSpec as P

HEAD_SIZE = 128
CORES = 2
LANES = 128


EPS = 1e-05
ADAPTER_SCALE = 2.0
F32 = jnp.float32
BF16 = jnp.bfloat16
NT = (((1,), (1,)), ((), ()))
NN = (((1,), (0,)), ((), ()))


def from_behind(block, axis, distance):
    devices = range(lax.axis_size(axis))
    route = [((i - distance) % len(devices), i) for i in devices]
    return lax.ppermute(block, axis, route)


def dot(left, right, dims):
    return lax.dot_general(left, right, dims, preferred_element_type=F32)


def prologue_kernel(x_ref, scale_ref, down_ref, fv_ref, vup_ref, inv_ref, mid_ref, value_ref):
    width = x_ref.shape[1]
    rank = vup_ref.shape[0]
    hidden = x_ref[...].astype(F32)
    inverse = lax.rsqrt(jnp.sum(hidden * hidden, axis=-1, keepdims=True) * (1.0 / width) + EPS)
    inv_ref[...] = inverse
    normed = (hidden * inverse * scale_ref[...].astype(F32)).astype(BF16)
    mid = dot(normed, down_ref[...], NT).astype(BF16)
    mid_ref[...] = mid
    value_mid = mid[:, rank:] * ADAPTER_SCALE
    value_ref[...] = (
        fv_ref[...].astype(F32) + dot(value_mid.astype(BF16), vup_ref[...], NN)
    ).astype(BF16)


def prologue(x, scale, down, frozen_values, vup, steps):
    rows, width = x.shape
    block = rows // steps
    kv = frozen_values.shape[1]
    ranks = down.shape[0]
    whole = lambda i: (0, 0)
    by_rows = lambda i: (i, 0)
    return pl.pallas_call(
        prologue_kernel,
        grid=(steps,),
        in_specs=[
            pl.BlockSpec((block, width), by_rows),
            pl.BlockSpec((1, width), whole),
            pl.BlockSpec((ranks, width), whole),
            pl.BlockSpec((block, kv), by_rows),
            pl.BlockSpec(vup.shape, whole),
        ],
        out_specs=[
            pl.BlockSpec((block, 1), by_rows),
            pl.BlockSpec((block, ranks), by_rows),
            pl.BlockSpec((block, kv), by_rows),
        ],
        out_shape=[
            jax.ShapeDtypeStruct((rows, 1), F32),
            jax.ShapeDtypeStruct((rows, ranks), BF16),
            jax.ShapeDtypeStruct((rows, kv), BF16),
        ],
        cost_estimate=pl.CostEstimate(
            flops=40 * rows * width, bytes_accessed=2 * rows * width, transcendentals=0
        ),
        name="prologue",
    )(x, scale, down, frozen_values, vup)


def attention_kernel(
    order_ref,
    fq_ref,
    grad_ref,
    key_ref,
    prior_key_ref,
    value_ref,
    prior_value_ref,
    mid_ref,
    mid_t_ref,
    up_ref,
    dv_ref,
    dv_prior_ref,
    qb_ref,
    dq_mid_ref,
):
    head = pl.program_id(0)
    rows = fq_ref.shape[0]
    heads = fq_ref.shape[1] // HEAD_SIZE
    rank = up_ref.shape[0]
    factor = 1.0 / math.sqrt(HEAD_SIZE)
    displaced = order_ref[0] == head
    for i in range(1, order_ref.shape[0] // 2):
        displaced = jnp.logical_or(displaced, order_ref[i] == head)
    odd = lax.rem(lax.axis_index("seq"), 2) == 1
    needs_prior = jnp.logical_xor(displaced, odd)

    @pl.when(head == 0)
    def _():
        dq_mid_ref[...] = jnp.zeros_like(dq_mid_ref)

    def run(with_prior):
        keys = key_ref[...]
        values = value_ref[...]
        if with_prior:
            keys = jnp.concatenate([keys, prior_key_ref[...]], axis=0)
            values = jnp.concatenate([values, prior_value_ref[...]], axis=0)
        keys_t = keys.T
        query_mid = mid_ref[:, :rank] * ADAPTER_SCALE
        mid_t = (mid_t_ref[:rank] * ADAPTER_SCALE).astype(BF16)
        key_pos = lax.broadcasted_iota(jnp.int32, (rows, rows), 0)
        query_pos = lax.broadcasted_iota(jnp.int32, (rows, rows), 1)
        causal = key_pos <= query_pos
        dv = None
        dq_mid = dq_mid_ref[...]
        for j in range(heads):
            cols = slice(j * HEAD_SIZE, (j + 1) * HEAD_SIZE)
            up = up_ref[:, cols]
            query = (
                fq_ref[:, cols].astype(F32) + dot(query_mid.astype(BF16), up, NN)
            ).astype(BF16)
            grad = grad_ref[:, cols]
            scores = dot(keys, query, NT)
            own = jnp.where(causal, scores[:rows], -jnp.inf)
            if with_prior:
                scores = jnp.concatenate([own, scores[rows:]], axis=0)
            else:
                scores = own
            top = jnp.max(scores, axis=0, keepdims=True)
            exponent = jnp.exp2((scores - top) * (factor * math.log2(math.e)))
            probs = exponent * (1.0 / jnp.sum(exponent, axis=0, keepdims=True))
            weights = probs.astype(BF16)
            dprob = dot(values, grad, NT)
            delta = jnp.sum(weights.astype(F32) * dprob, axis=0, keepdims=True)
            dscore = (probs * (dprob - delta)).astype(BF16)
            term = dot(weights, grad, NN)
            dv = term if dv is None else dv + term
            dquery = (dot(keys_t, dscore, NN) * factor).astype(BF16)
            qb_ref[:, cols] = dot(mid_t, dquery, NT)
            dq_mid = dq_mid + dot(up, dquery, NN)
        dq_mid_ref[...] = dq_mid
        dv_ref[...] = dv[:rows]
        if with_prior:
            dv_prior_ref[...] = dv[rows:].astype(BF16)
        else:
            dv_prior_ref[...] = jnp.zeros_like(dv_prior_ref)

    @pl.when(needs_prior)
    def _():
        run(True)

    @pl.when(jnp.logical_not(needs_prior))
    def _():
        run(False)


def attention(order, fq, grads, keys, prior_keys, values, prior_values, mid, mid_t, up):
    rows, queries = fq.shape
    kv = keys.shape[1]
    kv_heads = kv // HEAD_SIZE
    wide = queries // kv_heads
    rank = up.shape[0]
    by_head = lambda h, order: (0, h)
    whole = lambda h, order: (0, 0)
    narrow = pl.BlockSpec((rows, HEAD_SIZE), by_head)
    broad = pl.BlockSpec((rows, wide), by_head)
    return pl.pallas_call(
        attention_kernel,
        grid_spec=pltpu.PrefetchScalarGridSpec(
            num_scalar_prefetch=1,
            grid=(kv_heads,),
            in_specs=[
                broad,
                broad,
                narrow,
                narrow,
                narrow,
                narrow,
                pl.BlockSpec(mid.shape, whole),
                pl.BlockSpec(mid_t.shape, whole),
                pl.BlockSpec((rank, wide), by_head),
            ],
            out_specs=[
                narrow,
                narrow,
                pl.BlockSpec((rank, wide), by_head),
                pl.BlockSpec((rank, rows), whole),
            ],
        ),
        out_shape=[
            jax.ShapeDtypeStruct((rows, kv), F32),
            jax.ShapeDtypeStruct((rows, kv), BF16),
            jax.ShapeDtypeStruct((rank, queries), F32),
            jax.ShapeDtypeStruct((rank, rows), F32),
        ],
        cost_estimate=pl.CostEstimate(
            flops=12 * rows * rows * queries,
            bytes_accessed=4 * rows * queries,
            transcendentals=0,
        ),
        name="attention",
    )(order, fq, grads, keys, prior_keys, values, prior_values, mid, mid_t, up)


def epilogue_kernel(
    x_ref,
    inv_ref,
    scale_ref,
    down_ref,
    dq_mid_ref,
    dv_ref,
    handed_ref,
    vup_ref,
    mid_t_ref,
    qb_ref,
    packed_ref,
    inner_ref,
    gain_ref,
):
    step = pl.program_id(0)
    block = x_ref.shape[1]
    rank = vup_ref.shape[0]
    width = block * pl.num_programs(0)
    full = gain_ref.shape[0] * block
    queries = qb_ref.shape[1]
    kv = dv_ref.shape[1]

    @pl.when(step == 0)
    def _():
        dv = (dv_ref[...] + handed_ref[...].astype(F32)).astype(BF16)
        mid_t = (mid_t_ref[rank:] * ADAPTER_SCALE).astype(BF16)
        packed_ref[:, 2 * full : 2 * full + queries] = qb_ref[...].astype(BF16)
        packed_ref[:, 2 * full + queries : 2 * full + queries + kv] = dot(mid_t, dv, NN).astype(
            BF16
        )
        dv_mid = dot(vup_ref[...], dv, NT)
        inner_ref[...] = (
            ADAPTER_SCALE * jnp.concatenate([dq_mid_ref[...], dv_mid], axis=0)
        ).astype(BF16)
        gain_ref[...] = jnp.zeros_like(gain_ref)
        used = 2 * full + queries + kv + block
        if used < packed_ref.shape[1]:
            packed_ref[:, used:] = jnp.zeros((rank, packed_ref.shape[1] - used), BF16)

    inner = inner_ref[...]
    unit = x_ref[...].astype(F32) * inv_ref[...]
    normed = (unit * scale_ref[...].astype(F32)).astype(BF16)
    raw = dot(inner, normed, NN).astype(BF16)
    at = pl.multiple_of(step * block, block)
    packed_ref[:, pl.ds(at, block)] = raw[:rank]
    packed_ref[:, pl.ds(at + full, block)] = raw[rank:]
    gain = jnp.sum(
        down_ref[...].astype(F32) * dot(inner, unit.astype(BF16), NN), axis=0, keepdims=True
    )
    row = lax.broadcasted_iota(jnp.int32, gain_ref.shape, 0)
    gain_ref[...] = jnp.where(row == step, gain, gain_ref[...])

    @pl.when(step == pl.num_programs(0) - 1)
    def _():
        base = 2 * full + queries + kv
        packed_ref[:, base : base + block] = gain_ref[...].astype(BF16)


def epilogue(x, inverse, scale, down, dq_mid, dv, handed, vup, mid_t, qb, total):
    rows, width = x.shape
    rank = vup.shape[0]
    block = width // rank
    whole = lambda j: (0, 0)
    by_cols = lambda j: (0, j)
    kept = lambda a: pl.BlockSpec(a.shape, whole)
    return pl.pallas_call(
        epilogue_kernel,
        grid=(rank,),
        in_specs=[
            pl.BlockSpec((rows, block), by_cols),
            kept(inverse),
            pl.BlockSpec((1, block), by_cols),
            pl.BlockSpec((down.shape[0], block), by_cols),
            kept(dq_mid),
            kept(dv),
            kept(handed),
            kept(vup),
            kept(mid_t),
            kept(qb),
        ],
        out_specs=pl.BlockSpec((rank, total), whole),
        out_shape=jax.ShapeDtypeStruct((rank, total), BF16),
        scratch_shapes=[
            pltpu.VMEM((2 * rank, rows), BF16),
            pltpu.VMEM((rank, block), F32),
        ],
        cost_estimate=pl.CostEstimate(
            flops=80 * rows * width, bytes_accessed=2 * rows * width, transcendentals=0
        ),
        name="epilogue",
    )(x, inverse, scale, down, dq_mid, dv, handed, vup, mid_t, qb)


def reduce_kernel(
    seqs,
    planes,
    limit,
    packed_ref,
    qa_ref,
    qb_ref,
    va_ref,
    vb_ref,
    gain_ref,
    parts,
    column,
    full,
    send_one,
    recv_one,
    send_two,
    recv_two,
    send_three,
    recv_three,
):
    group = seqs * CORES
    piece = full.shape[1] // group
    place = lax.axis_index("dp")
    plane = place // CORES
    me = lax.axis_index("seq") * CORES + place % CORES

    def in_group(k):
        peer = lax.rem(me + k, group)
        return peer, {"seq": peer // CORES, "dp": plane * CORES + peer % CORES}

    def in_column(k):
        return {"dp": lax.rem(plane + k, planes) * CORES + place % CORES}

    def span(index):
        return pl.ds(pl.multiple_of(index * piece, piece), piece)

    barrier = pltpu.get_barrier_semaphore()
    for k in range(1, group):
        pl.semaphore_signal(
            barrier, inc=1, device_id=in_group(k)[1], device_id_type=pl.DeviceIdType.MESH
        )
    for k in range(1, planes):
        pl.semaphore_signal(
            barrier, inc=1, device_id=in_column(k), device_id_type=pl.DeviceIdType.MESH
        )
    pl.semaphore_wait(barrier, group + planes - 2)

    def remote(source, target, send, recv, device):
        copy = pltpu.make_async_remote_copy(
            src_ref=source,
            dst_ref=target,
            send_sem=send,
            recv_sem=recv,
            device_id=device,
            device_id_type=pl.DeviceIdType.MESH,
        )
        copy.start()
        return copy

    first = []
    for k in range(1, group):
        peer, device = in_group(k)
        first.append(
            remote(
                packed_ref.at[:, span(peer)],
                parts.at[k - 1],
                send_one.at[k - 1],
                recv_one.at[k - 1],
                device,
            )
        )
    total = packed_ref[:, span(me)].astype(F32)
    for k in range(1, group):
        first[k - 1].wait_recv()
        total = total + parts[k - 1].astype(F32)
    column[plane] = total.astype(BF16)
    second = [
        remote(
            column.at[plane],
            column.at[plane],
            send_two.at[k - 1],
            recv_two.at[k - 1],
            in_column(k),
        )
        for k in range(1, planes)
    ]
    for copy in second:
        copy.wait_recv()
    total = column[0].astype(F32)
    for i in range(1, planes):
        total = total + column[i].astype(F32)
    full[:, span(me)] = total.astype(BF16)
    third = [
        remote(
            full.at[:, span(me)],
            full.at[:, span(me)],
            send_three.at[k - 1],
            recv_three.at[k - 1],
            in_group(k)[1],
        )
        for k in range(1, group)
    ]
    for copy in third:
        copy.wait_recv()
    for copy in first + second + third:
        copy.wait_send()
    sums = full[...].astype(F32)
    squares = jnp.sum(jnp.sum(sums * sums, axis=1, keepdims=True), axis=0, keepdims=True)
    scale = jnp.minimum(1.0, limit / jnp.sqrt(squares))
    at = 0
    for out in (qa_ref, va_ref, qb_ref, vb_ref, gain_ref):
        out[...] = full[:, at : at + out.shape[1]].astype(F32) * scale
        at += out.shape[1]


def reduced(packed, seqs, planes, limit, widths):
    rank, total = packed.shape
    group = seqs * CORES
    piece = total // group
    vmem = pl.BlockSpec(memory_space=pltpu.VMEM)
    dma = pltpu.SemaphoreType.DMA
    return pl.pallas_call(
        functools.partial(reduce_kernel, seqs, planes, limit),
        in_specs=[vmem],
        out_specs=[vmem] * len(widths),
        out_shape=[jax.ShapeDtypeStruct((rank, w), F32) for w in widths],
        scratch_shapes=[
            pltpu.VMEM((group - 1, rank, piece), BF16),
            pltpu.VMEM((planes, rank, piece), BF16),
            pltpu.VMEM((rank, total), BF16),
            dma((group - 1,)),
            dma((group - 1,)),
            dma((max(planes - 1, 1),)),
            dma((max(planes - 1, 1),)),
            dma((group - 1,)),
            dma((group - 1,)),
        ],
        compiler_params=pltpu.CompilerParams(collective_id=0, has_side_effects=True),
        name="reduced",
    )(packed)


def shards(
    layer_input,
    frozen_queries,
    frozen_keys,
    frozen_values,
    output_gradient,
    norm_scale_vector,
    query_down_weight,
    query_up_weight,
    value_down_weight,
    value_up_weight,
    head_ordering,
):
    seqs = lax.axis_size("seq")
    planes = lax.axis_size("dp") // CORES
    rank, width = query_down_weight.shape
    queries = query_up_weight.shape[1]
    kv = value_up_weight.shape[1]
    scale = norm_scale_vector.reshape(1, width)
    down = jnp.concatenate([query_down_weight, value_down_weight], axis=0)
    keys = frozen_keys[0]
    prior_keys = from_behind(keys, "seq", 1)
    inverse, mid, values = prologue(
        layer_input[0], scale, down, frozen_values[0], value_up_weight, 4
    )
    mid_t = mid.T
    prior_values = from_behind(values, "seq", 1)
    dv, dv_prior, qb, dq_mid = attention(
        head_ordering,
        frozen_queries[0],
        output_gradient[0],
        keys,
        prior_keys,
        values,
        prior_values,
        mid,
        mid_t,
        query_up_weight,
    )
    handed = from_behind(dv_prior, "seq", -1)
    used = 2 * width + queries + kv + width // rank
    unit = seqs * CORES * LANES
    total = -(-used // unit) * unit
    packed = epilogue(
        layer_input[0], inverse, scale, down, dq_mid, dv, handed, value_up_weight, mid_t, qb, total
    )
    limit = math.sqrt(rank * (2 * width + queries + kv) + width)
    qa, gqb, va, vb, gain = reduced(
        packed, seqs, planes, limit, (width, queries, width, kv, width // rank)
    )
    return (qa, gqb, va, vb, gain.reshape(width))


def solution(mesh):
    placed = (
        P("dp", "seq", None),
        P("dp", "seq", None),
        P("dp", "seq", None),
        P("dp", "seq", None),
        P("dp", "seq", None),
        P(),
        P(),
        P(),
        P(),
        P(),
        P(),
    )
    return jax.shard_map(
        shards, mesh=mesh, in_specs=placed, out_specs=(P(), P(), P(), P(), P()), check_vma=False
    )
```

```python
import functools
import math

import jax
import jax.numpy as jnp
from jax import lax
from jax.experimental import pallas as pl
from jax.experimental.pallas import tpu as pltpu
from jax.sharding import PartitionSpec as P

HEAD_SIZE = 128
CORES = 2
LANES = 128


EPS = 1e-05
ADAPTER_SCALE = 2.0
F32 = jnp.float32
BF16 = jnp.bfloat16
NT = (((1,), (1,)), ((), ()))
NN = (((1,), (0,)), ((), ()))


def from_behind(block, axis, distance):
    devices = range(lax.axis_size(axis))
    route = [((i - distance) % len(devices), i) for i in devices]
    return lax.ppermute(block, axis, route)


def dot(left, right, dims):
    return lax.dot_general(left, right, dims, preferred_element_type=F32)


def scaled(block, scale_ref, first, chunks):
    scale = scale_ref[pl.ds(first, chunks), :].astype(F32)
    return jnp.concatenate(
        [
            (block[:, i * LANES : (i + 1) * LANES] * scale[i : i + 1]).astype(BF16)
            for i in range(chunks)
        ],
        axis=1,
    )


def flipped(columns, start, count):
    rows = lax.broadcasted_iota(jnp.int32, (count, columns.shape[1]), 0)
    cols = lax.broadcasted_iota(jnp.int32, (count, columns.shape[1]), 1)
    pick = jnp.where(rows + start == cols, ADAPTER_SCALE, 0.0).astype(BF16)
    return dot(pick, columns, NT).astype(BF16)


def prologue_kernel(
    heads_ref,
    x_ref,
    scale_ref,
    qdown_ref,
    vdown_ref,
    fv_ref,
    vup_ref,
    inv_ref,
    qmid_ref,
    vmid_ref,
    value_ref,
    given_ref,
):
    width = x_ref.shape[1]
    hidden = x_ref[...].astype(F32)
    inverse = lax.rsqrt(jnp.sum(hidden * hidden, axis=-1, keepdims=True) * (1.0 / width) + EPS)
    inv_ref[...] = inverse
    normed = scaled(hidden * inverse, scale_ref, 0, width // LANES)
    qmid_ref[...] = dot(normed, qdown_ref[...], NT).astype(BF16)
    value_mid = dot(normed, vdown_ref[...], NT).astype(BF16)
    vmid_ref[...] = value_mid
    value_ref[...] = (
        fv_ref[...].astype(F32) + dot((value_mid * ADAPTER_SCALE).astype(BF16), vup_ref[...], NN)
    ).astype(BF16)
    half = given_ref.shape[1] // HEAD_SIZE
    for i in range(half):
        at = pl.multiple_of(heads_ref[half + i] * HEAD_SIZE, HEAD_SIZE)
        given_ref[:, i * HEAD_SIZE : (i + 1) * HEAD_SIZE] = value_ref[:, pl.ds(at, HEAD_SIZE)]


def prologue(heads, x, scale, qdown, vdown, frozen_values, vup, steps):
    rows, width = x.shape
    block = rows // steps
    kv = frozen_values.shape[1]
    rank = qdown.shape[0]
    whole = lambda i, heads: (0, 0)
    by_rows = lambda i, heads: (i, 0)
    return pl.pallas_call(
        prologue_kernel,
        grid_spec=pltpu.PrefetchScalarGridSpec(
            num_scalar_prefetch=1,
            grid=(steps,),
            in_specs=[
                pl.BlockSpec((block, width), by_rows),
                pl.BlockSpec(scale.shape, whole),
                pl.BlockSpec(qdown.shape, whole),
                pl.BlockSpec(vdown.shape, whole),
                pl.BlockSpec((block, kv), by_rows),
                pl.BlockSpec(vup.shape, whole),
            ],
            out_specs=[
                pl.BlockSpec((block, 1), by_rows),
                pl.BlockSpec((block, rank), by_rows),
                pl.BlockSpec((block, rank), by_rows),
                pl.BlockSpec((block, kv), by_rows),
                pl.BlockSpec((block, kv // 2), by_rows),
            ],
        ),
        out_shape=[
            jax.ShapeDtypeStruct((rows, 1), F32),
            jax.ShapeDtypeStruct((rows, rank), BF16),
            jax.ShapeDtypeStruct((rows, rank), BF16),
            jax.ShapeDtypeStruct((rows, kv), BF16),
            jax.ShapeDtypeStruct((rows, kv // 2), BF16),
        ],
        cost_estimate=pl.CostEstimate(
            flops=40 * rows * width, bytes_accessed=2 * rows * width, transcendentals=0
        ),
        name="prologue",
    )(heads, x, scale, qdown, vdown, frozen_values, vup)


def attention_kernel(has_start, with_prior, heads_ref, *refs):
    refs = list(refs)
    fq_ref, grad_ref, key_ref, value_ref, mid_ref, up_ref = refs[:6]
    refs = refs[6:]
    if has_start:
        start_ref = refs.pop(0)
    if with_prior:
        prior_key_ref, prior_value_ref = refs.pop(0), refs.pop(0)
    dv_ref, qb_ref, dq_mid_ref = refs[:3]
    rows = fq_ref.shape[0]
    heads = fq_ref.shape[1] // HEAD_SIZE
    rank = up_ref.shape[0]
    factor = 1.0 / math.sqrt(HEAD_SIZE)

    @pl.when(pl.program_id(0) == 0)
    def _():
        dq_mid_ref[...] = start_ref[...] if has_start else jnp.zeros_like(dq_mid_ref)

    keys = key_ref[...]
    values = value_ref[...]
    if with_prior:
        keys = jnp.concatenate([keys, prior_key_ref[...]], axis=0)
        values = jnp.concatenate([values, prior_value_ref[...]], axis=0)
    keys_t = keys.T
    query_mid = (mid_ref[...] * ADAPTER_SCALE).astype(BF16)
    mid_t = flipped(mid_ref[...], 0, rank)
    key_pos = lax.broadcasted_iota(jnp.int32, (rows, rows), 0)
    query_pos = lax.broadcasted_iota(jnp.int32, (rows, rows), 1)
    causal = key_pos <= query_pos
    dv = None
    dq_mid = dq_mid_ref[...]
    for j in range(heads):
        cols = slice(j * HEAD_SIZE, (j + 1) * HEAD_SIZE)
        up = up_ref[:, cols]
        query = (fq_ref[:, cols].astype(F32) + dot(query_mid, up, NN)).astype(BF16)
        grad = grad_ref[:, cols]
        scores = dot(keys, query, NT)
        own = jnp.where(causal, scores[:rows], -jnp.inf)
        scores = jnp.concatenate([own, scores[rows:]], axis=0) if with_prior else own
        top = jnp.max(scores, axis=0, keepdims=True)
        exponent = jnp.exp2((scores - top) * (factor * math.log2(math.e)))
        probs = exponent * (1.0 / jnp.sum(exponent, axis=0, keepdims=True))
        weights = probs.astype(BF16)
        dprob = dot(values, grad, NT)
        delta = jnp.sum(weights.astype(F32) * dprob, axis=0, keepdims=True)
        dscore = (probs * (dprob - delta)).astype(BF16)
        term = dot(weights, grad, NN)
        dv = term if dv is None else dv + term
        dquery = (dot(keys_t, dscore, NN) * factor).astype(BF16)
        qb_ref[:, cols] = dot(mid_t, dquery, NT)
        dq_mid = dq_mid + dot(up, dquery, NN)
    dq_mid_ref[...] = dq_mid
    dv_ref[...] = dv[:rows]
    if with_prior:
        refs[3][...] = dv[rows:].astype(BF16)


def attention(first, count, heads, fq, grads, keys, values, mid, up, start, prior):
    rows, queries = fq.shape
    kv_heads = keys.shape[1] // HEAD_SIZE
    wide = queries // kv_heads
    rank = up.shape[0]
    by_head = lambda i, heads: (0, heads[first + i])
    by_slot = lambda i, heads: (0, i)
    whole = lambda i, heads: (0, 0)
    narrow = pl.BlockSpec((rows, HEAD_SIZE), by_head)
    broad = pl.BlockSpec((rows, wide), by_head)
    slot = pl.BlockSpec((rows, HEAD_SIZE), by_slot)
    operands = [fq, grads, keys, values, mid, up]
    in_specs = [
        broad,
        broad,
        narrow,
        narrow,
        pl.BlockSpec(mid.shape, whole),
        pl.BlockSpec((rank, wide), by_head),
    ]
    out_specs = [
        slot,
        pl.BlockSpec((rank, wide), by_slot),
        pl.BlockSpec((rank, rows), whole),
    ]
    out_shape = [
        jax.ShapeDtypeStruct((rows, count * HEAD_SIZE), F32),
        jax.ShapeDtypeStruct((rank, count * wide), F32),
        jax.ShapeDtypeStruct((rank, rows), F32),
    ]
    if start is not None:
        operands.append(start)
        in_specs.append(pl.BlockSpec(start.shape, whole))
    if prior is not None:
        operands += list(prior)
        in_specs += [narrow, slot]
        out_specs.append(slot)
        out_shape.append(jax.ShapeDtypeStruct((rows, count * HEAD_SIZE), BF16))
    return pl.pallas_call(
        functools.partial(attention_kernel, start is not None, prior is not None),
        grid_spec=pltpu.PrefetchScalarGridSpec(
            num_scalar_prefetch=1, grid=(count,), in_specs=in_specs, out_specs=out_specs
        ),
        out_shape=out_shape,
        cost_estimate=pl.CostEstimate(
            flops=count * 24 * rows * rows * wide,
            bytes_accessed=count * 4 * rows * wide,
            transcendentals=0,
        ),
        name="attention",
    )(heads, *operands)


def epilogue_kernel(
    counts,
    heads_ref,
    x_ref,
    inv_ref,
    scale_ref,
    qdown_ref,
    vdown_ref,
    dq_mid_ref,
    handed_ref,
    vup_ref,
    vmid_ref,
    *refs,
):
    dv_refs, qb_refs = refs[: len(counts)], refs[len(counts) : 2 * len(counts)]
    packed_ref, inner_ref, gain_ref = refs[2 * len(counts) :]
    step = pl.program_id(0)
    block = x_ref.shape[1]
    rank = vup_ref.shape[0]
    full = gain_ref.shape[0] * block
    kv = vup_ref.shape[1]
    half = handed_ref.shape[1] // HEAD_SIZE
    wide = qb_refs[0].shape[1] // counts[0][1]
    queries = kv // HEAD_SIZE * wide
    base = 2 * full + queries

    @pl.when(step == 0)
    def _():
        mid_t = flipped(vmid_ref[...], 0, rank)
        dv_mid = jnp.zeros(dq_mid_ref.shape, F32)
        for (first, count), dv_ref, qb_ref in zip(counts, dv_refs, qb_refs):
            for i in range(count):
                cols = slice(i * HEAD_SIZE, (i + 1) * HEAD_SIZE)
                dv = dv_ref[:, cols]
                if first + i >= half:
                    given = first + i - half
                    other = handed_ref[:, given * HEAD_SIZE : (given + 1) * HEAD_SIZE]
                    dv = dv + other.astype(F32)
                dv = dv.astype(BF16)
                head = heads_ref[first + i]
                at = pl.multiple_of(head * HEAD_SIZE, HEAD_SIZE)
                dv_mid = dv_mid + dot(vup_ref[:, pl.ds(at, HEAD_SIZE)], dv, NT)
                at = pl.multiple_of(base + head * HEAD_SIZE, HEAD_SIZE)
                packed_ref[:, pl.ds(at, HEAD_SIZE)] = dot(mid_t, dv, NN).astype(BF16)
                at = pl.multiple_of(2 * full + head * wide, HEAD_SIZE)
                packed_ref[:, pl.ds(at, wide)] = qb_ref[:, i * wide : (i + 1) * wide].astype(BF16)
        inner_ref[...] = (
            ADAPTER_SCALE * jnp.concatenate([dq_mid_ref[...], dv_mid], axis=0)
        ).astype(BF16)
        gain_ref[...] = jnp.zeros_like(gain_ref)
        used = base + kv + block
        if used < packed_ref.shape[1]:
            packed_ref[:, used:] = jnp.zeros((rank, packed_ref.shape[1] - used), BF16)

    inner = inner_ref[...]
    unit = x_ref[...].astype(F32) * inv_ref[...]
    normed = scaled(unit, scale_ref, 0, block // LANES)
    raw = dot(inner, normed, NN).astype(BF16)
    at = pl.multiple_of(step * block, block)
    packed_ref[:, pl.ds(at, block)] = raw[:rank]
    packed_ref[:, pl.ds(at + full, block)] = raw[rank:]
    spread = dot(inner, unit.astype(BF16), NN)
    gain = jnp.sum(
        qdown_ref[...].astype(F32) * spread[:rank] + vdown_ref[...].astype(F32) * spread[rank:],
        axis=0,
        keepdims=True,
    )
    row = lax.broadcasted_iota(jnp.int32, gain_ref.shape, 0)
    gain_ref[...] = jnp.where(row == step, gain, gain_ref[...])

    @pl.when(step == pl.num_programs(0) - 1)
    def _():
        packed_ref[:, base + kv : base + kv + block] = gain_ref[...].astype(BF16)


def epilogue(heads, counts, x, inverse, scale, qdown, vdown, dq_mid, handed, vup, vmid, dvs, qbs, total):
    rows, width = x.shape
    rank = vup.shape[0]
    block = width // rank
    whole = lambda j, heads: (0, 0)
    by_cols = lambda j, heads: (0, j)
    kept = lambda a: pl.BlockSpec(a.shape, whole)
    return pl.pallas_call(
        functools.partial(epilogue_kernel, counts),
        grid_spec=pltpu.PrefetchScalarGridSpec(
            num_scalar_prefetch=1,
            grid=(rank,),
            in_specs=[
                pl.BlockSpec((rows, block), by_cols),
                kept(inverse),
                pl.BlockSpec((block // LANES, LANES), lambda j, heads: (j, 0)),
                pl.BlockSpec((rank, block), by_cols),
                pl.BlockSpec((rank, block), by_cols),
                kept(dq_mid),
                kept(handed),
                kept(vup),
                kept(vmid),
            ]
            + [kept(a) for a in (*dvs, *qbs)],
            out_specs=pl.BlockSpec((rank, total), whole),
            scratch_shapes=[
                pltpu.VMEM((2 * rank, rows), BF16),
                pltpu.VMEM((rank, block), F32),
            ],
        ),
        out_shape=jax.ShapeDtypeStruct((rank, total), BF16),
        cost_estimate=pl.CostEstimate(
            flops=80 * rows * width, bytes_accessed=2 * rows * width, transcendentals=0
        ),
        name="epilogue",
    )(heads, x, inverse, scale, qdown, vdown, dq_mid, handed, vup, vmid, *dvs, *qbs)


def finish_kernel(limit, full_ref, qa_ref, qb_ref, va_ref, vb_ref, gain_ref):
    sums = full_ref[...].astype(F32)
    squares = jnp.sum(jnp.sum(sums * sums, axis=1, keepdims=True), axis=0, keepdims=True)
    scale = jnp.minimum(1.0, limit / jnp.sqrt(squares))
    at = 0
    for out in (qa_ref, va_ref, qb_ref, vb_ref):
        out[...] = full_ref[:, at : at + out.shape[1]].astype(F32) * scale
        at += out.shape[1]
    rank = full_ref.shape[0]
    chunks = gain_ref.shape[0] // rank
    for c in range(chunks):
        piece = full_ref[:, at + c * LANES : at + (c + 1) * LANES].astype(F32) * scale
        gain_ref[pl.ds(c, rank, stride=chunks), :] = piece


def finished(full, limit, widths, width):
    rank = full.shape[0]
    vmem = pl.BlockSpec(memory_space=pltpu.VMEM)
    return pl.pallas_call(
        functools.partial(finish_kernel, limit),
        in_specs=[vmem],
        out_specs=[vmem] * (len(widths) + 1),
        out_shape=[jax.ShapeDtypeStruct((rank, w), F32) for w in widths]
        + [jax.ShapeDtypeStruct((width // LANES, LANES), F32)],
        name="finished",
    )(full)


def reduce_kernel(
    seqs,
    planes,
    packed_ref,
    full,
    parts,
    column,
    send_one,
    recv_one,
    send_two,
    recv_two,
    send_three,
    recv_three,
):
    group = seqs * CORES
    piece = full.shape[1] // group
    place = lax.axis_index("dp")
    plane = place // CORES
    me = lax.axis_index("seq") * CORES + place % CORES

    def in_group(k):
        peer = lax.rem(me + k, group)
        return peer, {"seq": peer // CORES, "dp": plane * CORES + peer % CORES}

    def in_column(k):
        return {"dp": lax.rem(plane + k, planes) * CORES + place % CORES}

    def span(index):
        return pl.ds(pl.multiple_of(index * piece, piece), piece)

    barrier = pltpu.get_barrier_semaphore()
    for k in range(1, group):
        pl.semaphore_signal(
            barrier, inc=1, device_id=in_group(k)[1], device_id_type=pl.DeviceIdType.MESH
        )
    for k in range(1, planes):
        pl.semaphore_signal(
            barrier, inc=1, device_id=in_column(k), device_id_type=pl.DeviceIdType.MESH
        )
    pl.semaphore_wait(barrier, group + planes - 2)

    def remote(source, target, send, recv, device):
        copy = pltpu.make_async_remote_copy(
            src_ref=source,
            dst_ref=target,
            send_sem=send,
            recv_sem=recv,
            device_id=device,
            device_id_type=pl.DeviceIdType.MESH,
        )
        copy.start()
        return copy

    first = []
    for k in range(1, group):
        peer, device = in_group(k)
        first.append(
            remote(
                packed_ref.at[:, span(peer)],
                parts.at[k - 1],
                send_one.at[k - 1],
                recv_one.at[k - 1],
                device,
            )
        )
    total = packed_ref[:, span(me)].astype(F32)
    for k in range(1, group):
        first[k - 1].wait_recv()
        total = total + parts[k - 1].astype(F32)
    column[plane] = total.astype(BF16)
    second = [
        remote(
            column.at[plane],
            column.at[plane],
            send_two.at[k - 1],
            recv_two.at[k - 1],
            in_column(k),
        )
        for k in range(1, planes)
    ]
    for copy in second:
        copy.wait_recv()
    total = column[0].astype(F32)
    for i in range(1, planes):
        total = total + column[i].astype(F32)
    full[:, span(me)] = total.astype(BF16)
    third = [
        remote(
            full.at[:, span(me)],
            full.at[:, span(me)],
            send_three.at[k - 1],
            recv_three.at[k - 1],
            in_group(k)[1],
        )
        for k in range(1, group)
    ]
    for copy in third:
        copy.wait_recv()
    for copy in first + second + third:
        copy.wait_send()


def reduced(packed, seqs, planes):
    rank, total = packed.shape
    group = seqs * CORES
    piece = total // group
    vmem = pl.BlockSpec(memory_space=pltpu.VMEM)
    dma = pltpu.SemaphoreType.DMA
    return pl.pallas_call(
        functools.partial(reduce_kernel, seqs, planes),
        in_specs=[vmem],
        out_specs=vmem,
        out_shape=jax.ShapeDtypeStruct((rank, total), BF16),
        scratch_shapes=[
            pltpu.VMEM((group - 1, rank, piece), BF16),
            pltpu.VMEM((planes, rank, piece), BF16),
            dma((group - 1,)),
            dma((group - 1,)),
            dma((max(planes - 1, 1),)),
            dma((max(planes - 1, 1),)),
            dma((group - 1,)),
            dma((group - 1,)),
        ],
        compiler_params=pltpu.CompilerParams(collective_id=0, has_side_effects=True),
        name="reduced",
    )(packed)


def shards(
    layer_input,
    frozen_queries,
    frozen_keys,
    frozen_values,
    output_gradient,
    norm_scale_vector,
    query_down_weight,
    query_up_weight,
    value_down_weight,
    value_up_weight,
    head_ordering,
):
    seqs = lax.axis_size("seq")
    planes = lax.axis_size("dp") // CORES
    rank, width = query_down_weight.shape
    queries = query_up_weight.shape[1]
    kv = value_up_weight.shape[1]
    half = head_ordering.shape[0] // 2
    odd = lax.axis_index("seq") % 2 == 1
    heads = jnp.where(odd, jnp.roll(head_ordering, -half), head_ordering)
    scale = norm_scale_vector.reshape(width // LANES, LANES)
    x, fq, grads, keys = layer_input[0], frozen_queries[0], output_gradient[0], frozen_keys[0]
    prior_keys = from_behind(keys, "seq", 1)
    inverse, qmid, vmid, values, given = prologue(
        heads, x, scale, query_down_weight, value_down_weight, frozen_values[0], value_up_weight, 4
    )
    prior_values = from_behind(given, "seq", 1)
    counts = ((half, half - 1), (0, half), (2 * half - 1, 1))
    attend = functools.partial(attention, heads=heads, fq=fq, grads=grads, keys=keys)
    attend = functools.partial(attend, values=values, mid=qmid, up=query_up_weight)
    dv_a, qb_a, dq_mid = attend(*counts[0], start=None, prior=None)
    dv_b, qb_b, dq_mid, dv_prior = attend(
        *counts[1], start=dq_mid, prior=(prior_keys, prior_values)
    )
    handed = from_behind(dv_prior, "seq", -1)
    dv_c, qb_c, dq_mid = attend(*counts[2], start=dq_mid, prior=None)
    used = 2 * width + queries + kv + width // rank
    unit = seqs * CORES * LANES
    total = -(-used // unit) * unit
    packed = epilogue(
        heads,
        counts,
        x,
        inverse,
        scale,
        query_down_weight,
        value_down_weight,
        dq_mid,
        handed,
        value_up_weight,
        vmid,
        (dv_a, dv_b, dv_c),
        (qb_a, qb_b, qb_c),
        total,
    )
    limit = math.sqrt(rank * (2 * width + queries + kv) + width)
    qa, gqb, va, vb, gain = finished(
        reduced(packed, seqs, planes), limit, (width, queries, width, kv), width
    )
    return (qa, gqb, va, vb, gain.reshape(width))


def solution(mesh):
    placed = (
        P("dp", "seq", None),
        P("dp", "seq", None),
        P("dp", "seq", None),
        P("dp", "seq", None),
        P("dp", "seq", None),
        P(),
        P(),
        P(),
        P(),
        P(),
        P(),
    )
    return jax.shard_map(
        shards, mesh=mesh, in_specs=placed, out_specs=(P(), P(), P(), P(), P()), check_vma=False
    )
```

```python
import functools
import math

import jax
import jax.numpy as jnp
from jax import lax
from jax.experimental import pallas as pl
from jax.experimental.pallas import tpu as pltpu
from jax.sharding import PartitionSpec as P

HEAD_SIZE = 128
CORES = 2
LANES = 128
TOGETHER = 8


EPS = 1e-05
ADAPTER_SCALE = 2.0
F32 = jnp.float32
BF16 = jnp.bfloat16
NT = (((1,), (1,)), ((), ()))
NN = (((1,), (0,)), ((), ()))


def from_behind(block, axis, distance):
    devices = range(lax.axis_size(axis))
    route = [((i - distance) % len(devices), i) for i in devices]
    return lax.ppermute(block, axis, route)


def dot(left, right, dims):
    return lax.dot_general(left, right, dims, preferred_element_type=F32)


def scaled(block, scale_ref, first, chunks):
    scale = scale_ref[pl.ds(first, chunks), :].astype(F32)
    return jnp.concatenate(
        [
            (block[:, i * LANES : (i + 1) * LANES] * scale[i : i + 1]).astype(BF16)
            for i in range(chunks)
        ],
        axis=1,
    )


def flipped(columns, start, count):
    rows = lax.broadcasted_iota(jnp.int32, (count, columns.shape[1]), 0)
    cols = lax.broadcasted_iota(jnp.int32, (count, columns.shape[1]), 1)
    pick = jnp.where(rows + start == cols, ADAPTER_SCALE, 0.0).astype(BF16)
    return dot(pick, columns, NT).astype(BF16)


def prologue_kernel(
    heads_ref,
    x_ref,
    scale_ref,
    qdown_ref,
    vdown_ref,
    fv_ref,
    vup_ref,
    inv_ref,
    qmid_ref,
    vmid_ref,
    value_ref,
    given_ref,
):
    width = x_ref.shape[1]
    hidden = x_ref[...].astype(F32)
    inverse = lax.rsqrt(jnp.sum(hidden * hidden, axis=-1, keepdims=True) * (1.0 / width) + EPS)
    inv_ref[...] = inverse
    normed = scaled(hidden * inverse, scale_ref, 0, width // LANES)
    qmid_ref[...] = dot(normed, qdown_ref[...], NT).astype(BF16)
    value_mid = dot(normed, vdown_ref[...], NT).astype(BF16)
    vmid_ref[...] = value_mid
    value_ref[...] = (
        fv_ref[...].astype(F32) + dot((value_mid * ADAPTER_SCALE).astype(BF16), vup_ref[...], NN)
    ).astype(BF16)
    half = given_ref.shape[1] // HEAD_SIZE
    for i in range(half):
        at = pl.multiple_of(heads_ref[half + i] * HEAD_SIZE, HEAD_SIZE)
        given_ref[:, i * HEAD_SIZE : (i + 1) * HEAD_SIZE] = value_ref[:, pl.ds(at, HEAD_SIZE)]


def prologue(heads, x, scale, qdown, vdown, frozen_values, vup, steps):
    rows, width = x.shape
    block = rows // steps
    kv = frozen_values.shape[1]
    rank = qdown.shape[0]
    whole = lambda i, heads: (0, 0)
    by_rows = lambda i, heads: (i, 0)
    return pl.pallas_call(
        prologue_kernel,
        grid_spec=pltpu.PrefetchScalarGridSpec(
            num_scalar_prefetch=1,
            grid=(steps,),
            in_specs=[
                pl.BlockSpec((block, width), by_rows),
                pl.BlockSpec(scale.shape, whole),
                pl.BlockSpec(qdown.shape, whole),
                pl.BlockSpec(vdown.shape, whole),
                pl.BlockSpec((block, kv), by_rows),
                pl.BlockSpec(vup.shape, whole),
            ],
            out_specs=[
                pl.BlockSpec((block, 1), by_rows),
                pl.BlockSpec((block, rank), by_rows),
                pl.BlockSpec((block, rank), by_rows),
                pl.BlockSpec((block, kv), by_rows),
                pl.BlockSpec((block, kv // 2), by_rows),
            ],
        ),
        out_shape=[
            jax.ShapeDtypeStruct((rows, 1), F32),
            jax.ShapeDtypeStruct((rows, rank), BF16),
            jax.ShapeDtypeStruct((rows, rank), BF16),
            jax.ShapeDtypeStruct((rows, kv), BF16),
            jax.ShapeDtypeStruct((rows, kv // 2), BF16),
        ],
        cost_estimate=pl.CostEstimate(
            flops=40 * rows * width, bytes_accessed=2 * rows * width, transcendentals=0
        ),
        name="prologue",
    )(heads, x, scale, qdown, vdown, frozen_values, vup)


def attention_kernel(has_start, with_prior, heads_ref, *refs):
    refs = list(refs)
    fq_ref, grad_ref, key_ref, value_ref, mid_ref, up_ref = refs[:6]
    refs = refs[6:]
    if has_start:
        start_ref = refs.pop(0)
    if with_prior:
        prior_key_ref, prior_value_ref = refs.pop(0), refs.pop(0)
    dv_ref, qb_ref, dq_mid_ref = refs[:3]
    rows = fq_ref.shape[0]
    heads = fq_ref.shape[1] // HEAD_SIZE
    rank = up_ref.shape[0]
    factor = 1.0 / math.sqrt(HEAD_SIZE)

    @pl.when(pl.program_id(0) == 0)
    def _():
        dq_mid_ref[...] = start_ref[...] if has_start else jnp.zeros_like(dq_mid_ref)

    keys = key_ref[...]
    values = value_ref[...]
    if with_prior:
        keys = jnp.concatenate([keys, prior_key_ref[...]], axis=0)
        values = jnp.concatenate([values, prior_value_ref[...]], axis=0)
    keys_t = keys.T
    query_mid = (mid_ref[...] * ADAPTER_SCALE).astype(BF16)
    mid_t = flipped(mid_ref[...], 0, rank)
    key_pos = lax.broadcasted_iota(jnp.int32, (rows, rows), 0)
    query_pos = lax.broadcasted_iota(jnp.int32, (rows, rows), 1)
    causal = key_pos <= query_pos
    together = math.gcd(heads, TOGETHER)
    up = up_ref[...]
    query = (fq_ref[...].astype(F32) + dot(query_mid, up, NN)).astype(BF16)
    dv = None
    dqueries = []
    for j in range(0, heads, together):
        stacked = lambda array: jnp.concatenate(
            [array[:, i * HEAD_SIZE : (i + 1) * HEAD_SIZE] for i in range(j, j + together)], axis=0
        )
        grad = stacked(grad_ref)
        scores = dot(keys, stacked(query), NT)
        own = jnp.concatenate(
            [
                jnp.where(causal, scores[:rows, i * rows : (i + 1) * rows], -jnp.inf)
                for i in range(together)
            ],
            axis=1,
        )
        scores = jnp.concatenate([own, scores[rows:]], axis=0) if with_prior else own
        top = jnp.max(scores, axis=0, keepdims=True)
        exponent = jnp.exp2((scores - top) * (factor * math.log2(math.e)))
        probs = exponent * (1.0 / jnp.sum(exponent, axis=0, keepdims=True))
        weights = probs.astype(BF16)
        dprob = dot(values, grad, NT)
        delta = jnp.sum(weights.astype(F32) * dprob, axis=0, keepdims=True)
        dscore = (probs * (dprob - delta)).astype(BF16)
        term = dot(weights, grad, NN)
        dv = term if dv is None else dv + term
        dquery = (dot(keys_t, dscore, NN) * factor).astype(BF16)
        dqueries += [dquery[:, i * rows : (i + 1) * rows] for i in range(together)]
    dquery = jnp.concatenate(dqueries, axis=0)
    qb_ref[...] = dot(mid_t, dquery, NT)
    dq_mid_ref[...] += dot(up, dquery, NN)
    dv_ref[...] = dv[:rows]
    if with_prior:
        refs[3][...] = dv[rows:].astype(BF16)


def attention(first, count, heads, fq, grads, keys, values, mid, up, start, prior):
    rows, queries = fq.shape
    kv_heads = keys.shape[1] // HEAD_SIZE
    wide = queries // kv_heads
    rank = up.shape[0]
    by_head = lambda i, heads: (0, heads[first + i])
    by_slot = lambda i, heads: (0, i)
    whole = lambda i, heads: (0, 0)
    narrow = pl.BlockSpec((rows, HEAD_SIZE), by_head)
    broad = pl.BlockSpec((rows, wide), by_head)
    slot = pl.BlockSpec((rows, HEAD_SIZE), by_slot)
    operands = [fq, grads, keys, values, mid, up]
    in_specs = [
        broad,
        broad,
        narrow,
        narrow,
        pl.BlockSpec(mid.shape, whole),
        pl.BlockSpec((rank, wide), by_head),
    ]
    out_specs = [
        slot,
        pl.BlockSpec((rank, wide), by_slot),
        pl.BlockSpec((rank, rows), whole),
    ]
    out_shape = [
        jax.ShapeDtypeStruct((rows, count * HEAD_SIZE), F32),
        jax.ShapeDtypeStruct((rank, count * wide), F32),
        jax.ShapeDtypeStruct((rank, rows), F32),
    ]
    if start is not None:
        operands.append(start)
        in_specs.append(pl.BlockSpec(start.shape, whole))
    if prior is not None:
        operands += list(prior)
        in_specs += [narrow, slot]
        out_specs.append(slot)
        out_shape.append(jax.ShapeDtypeStruct((rows, count * HEAD_SIZE), BF16))
    return pl.pallas_call(
        functools.partial(attention_kernel, start is not None, prior is not None),
        grid_spec=pltpu.PrefetchScalarGridSpec(
            num_scalar_prefetch=1, grid=(count,), in_specs=in_specs, out_specs=out_specs
        ),
        out_shape=out_shape,
        cost_estimate=pl.CostEstimate(
            flops=count * 24 * rows * rows * wide,
            bytes_accessed=count * 4 * rows * wide,
            transcendentals=0,
        ),
        name="attention",
    )(heads, *operands)


def epilogue_kernel(
    counts,
    heads_ref,
    x_ref,
    inv_ref,
    scale_ref,
    qdown_ref,
    vdown_ref,
    dq_mid_ref,
    handed_ref,
    vup_ref,
    vmid_ref,
    *refs,
):
    dv_refs, qb_refs = refs[: len(counts)], refs[len(counts) : 2 * len(counts)]
    packed_ref, inner_ref, gain_ref = refs[2 * len(counts) :]
    step = pl.program_id(0)
    block = x_ref.shape[1]
    rank = vup_ref.shape[0]
    full = gain_ref.shape[0] * block
    kv = vup_ref.shape[1]
    half = handed_ref.shape[1] // HEAD_SIZE
    wide = qb_refs[0].shape[1] // counts[0][1]
    queries = kv // HEAD_SIZE * wide
    base = 2 * full + queries

    @pl.when(step == 0)
    def _():
        mid_t = flipped(vmid_ref[...], 0, rank)
        dv_mid = jnp.zeros(dq_mid_ref.shape, F32)
        for (first, count), dv_ref, qb_ref in zip(counts, dv_refs, qb_refs):
            for i in range(count):
                cols = slice(i * HEAD_SIZE, (i + 1) * HEAD_SIZE)
                dv = dv_ref[:, cols]
                if first + i >= half:
                    given = first + i - half
                    other = handed_ref[:, given * HEAD_SIZE : (given + 1) * HEAD_SIZE]
                    dv = dv + other.astype(F32)
                dv = dv.astype(BF16)
                head = heads_ref[first + i]
                at = pl.multiple_of(head * HEAD_SIZE, HEAD_SIZE)
                dv_mid = dv_mid + dot(vup_ref[:, pl.ds(at, HEAD_SIZE)], dv, NT)
                at = pl.multiple_of(base + head * HEAD_SIZE, HEAD_SIZE)
                packed_ref[:, pl.ds(at, HEAD_SIZE)] = dot(mid_t, dv, NN).astype(BF16)
                at = pl.multiple_of(2 * full + head * wide, HEAD_SIZE)
                packed_ref[:, pl.ds(at, wide)] = qb_ref[:, i * wide : (i + 1) * wide].astype(BF16)
        inner_ref[...] = (
            ADAPTER_SCALE * jnp.concatenate([dq_mid_ref[...], dv_mid], axis=0)
        ).astype(BF16)
        gain_ref[...] = jnp.zeros_like(gain_ref)
        used = base + kv + block
        if used < packed_ref.shape[1]:
            packed_ref[:, used:] = jnp.zeros((rank, packed_ref.shape[1] - used), BF16)

    inner = inner_ref[...]
    unit = x_ref[...].astype(F32) * inv_ref[...]
    normed = scaled(unit, scale_ref, 0, block // LANES)
    raw = dot(inner, normed, NN).astype(BF16)
    at = pl.multiple_of(step * block, block)
    packed_ref[:, pl.ds(at, block)] = raw[:rank]
    packed_ref[:, pl.ds(at + full, block)] = raw[rank:]
    spread = dot(inner, unit.astype(BF16), NN)
    gain = jnp.sum(
        qdown_ref[...].astype(F32) * spread[:rank] + vdown_ref[...].astype(F32) * spread[rank:],
        axis=0,
        keepdims=True,
    )
    row = lax.broadcasted_iota(jnp.int32, gain_ref.shape, 0)
    gain_ref[...] = jnp.where(row == step, gain, gain_ref[...])

    @pl.when(step == pl.num_programs(0) - 1)
    def _():
        packed_ref[:, base + kv : base + kv + block] = gain_ref[...].astype(BF16)


def epilogue(heads, counts, x, inverse, scale, qdown, vdown, dq_mid, handed, vup, vmid, dvs, qbs, total):
    rows, width = x.shape
    rank = vup.shape[0]
    block = width // rank
    whole = lambda j, heads: (0, 0)
    by_cols = lambda j, heads: (0, j)
    kept = lambda a: pl.BlockSpec(a.shape, whole)
    return pl.pallas_call(
        functools.partial(epilogue_kernel, counts),
        grid_spec=pltpu.PrefetchScalarGridSpec(
            num_scalar_prefetch=1,
            grid=(rank,),
            in_specs=[
                pl.BlockSpec((rows, block), by_cols),
                kept(inverse),
                pl.BlockSpec((block // LANES, LANES), lambda j, heads: (j, 0)),
                pl.BlockSpec((rank, block), by_cols),
                pl.BlockSpec((rank, block), by_cols),
                kept(dq_mid),
                kept(handed),
                kept(vup),
                kept(vmid),
            ]
            + [kept(a) for a in (*dvs, *qbs)],
            out_specs=pl.BlockSpec((rank, total), whole),
            scratch_shapes=[
                pltpu.VMEM((2 * rank, rows), BF16),
                pltpu.VMEM((rank, block), F32),
            ],
        ),
        out_shape=jax.ShapeDtypeStruct((rank, total), BF16),
        cost_estimate=pl.CostEstimate(
            flops=80 * rows * width, bytes_accessed=2 * rows * width, transcendentals=0
        ),
        name="epilogue",
    )(heads, x, inverse, scale, qdown, vdown, dq_mid, handed, vup, vmid, *dvs, *qbs)


def finish_kernel(limit, full_ref, qa_ref, qb_ref, va_ref, vb_ref, gain_ref):
    sums = full_ref[...].astype(F32)
    squares = jnp.sum(jnp.sum(sums * sums, axis=1, keepdims=True), axis=0, keepdims=True)
    scale = jnp.minimum(1.0, limit / jnp.sqrt(squares))
    at = 0
    for out in (qa_ref, va_ref, qb_ref, vb_ref):
        out[...] = full_ref[:, at : at + out.shape[1]].astype(F32) * scale
        at += out.shape[1]
    rank = full_ref.shape[0]
    chunks = gain_ref.shape[0] // rank
    for c in range(chunks):
        piece = full_ref[:, at + c * LANES : at + (c + 1) * LANES].astype(F32) * scale
        gain_ref[pl.ds(c, rank, stride=chunks), :] = piece


def finished(full, limit, widths, width):
    rank = full.shape[0]
    vmem = pl.BlockSpec(memory_space=pltpu.VMEM)
    return pl.pallas_call(
        functools.partial(finish_kernel, limit),
        in_specs=[vmem],
        out_specs=[vmem] * (len(widths) + 1),
        out_shape=[jax.ShapeDtypeStruct((rank, w), F32) for w in widths]
        + [jax.ShapeDtypeStruct((width // LANES, LANES), F32)],
        name="finished",
    )(full)


def reduce_kernel(
    seqs,
    planes,
    packed_ref,
    full,
    parts,
    column,
    send_one,
    recv_one,
    send_two,
    recv_two,
    send_three,
    recv_three,
):
    group = seqs * CORES
    piece = full.shape[1] // group
    place = lax.axis_index("dp")
    plane = place // CORES
    me = lax.axis_index("seq") * CORES + place % CORES

    def in_group(k):
        peer = lax.rem(me + k, group)
        return peer, {"seq": peer // CORES, "dp": plane * CORES + peer % CORES}

    def in_column(k):
        return {"dp": lax.rem(plane + k, planes) * CORES + place % CORES}

    def span(index):
        return pl.ds(pl.multiple_of(index * piece, piece), piece)

    barrier = pltpu.get_barrier_semaphore()
    for k in range(1, group):
        pl.semaphore_signal(
            barrier, inc=1, device_id=in_group(k)[1], device_id_type=pl.DeviceIdType.MESH
        )
    for k in range(1, planes):
        pl.semaphore_signal(
            barrier, inc=1, device_id=in_column(k), device_id_type=pl.DeviceIdType.MESH
        )
    pl.semaphore_wait(barrier, group + planes - 2)

    def remote(source, target, send, recv, device):
        copy = pltpu.make_async_remote_copy(
            src_ref=source,
            dst_ref=target,
            send_sem=send,
            recv_sem=recv,
            device_id=device,
            device_id_type=pl.DeviceIdType.MESH,
        )
        copy.start()
        return copy

    first = []
    for k in range(1, group):
        peer, device = in_group(k)
        first.append(
            remote(
                packed_ref.at[:, span(peer)],
                parts.at[k - 1],
                send_one.at[k - 1],
                recv_one.at[k - 1],
                device,
            )
        )
    total = packed_ref[:, span(me)].astype(F32)
    for k in range(1, group):
        first[k - 1].wait_recv()
        total = total + parts[k - 1].astype(F32)
    column[plane] = total.astype(BF16)
    second = [
        remote(
            column.at[plane],
            column.at[plane],
            send_two.at[k - 1],
            recv_two.at[k - 1],
            in_column(k),
        )
        for k in range(1, planes)
    ]
    for copy in second:
        copy.wait_recv()
    total = column[0].astype(F32)
    for i in range(1, planes):
        total = total + column[i].astype(F32)
    full[:, span(me)] = total.astype(BF16)
    third = [
        remote(
            full.at[:, span(me)],
            full.at[:, span(me)],
            send_three.at[k - 1],
            recv_three.at[k - 1],
            in_group(k)[1],
        )
        for k in range(1, group)
    ]
    for copy in third:
        copy.wait_recv()
    for copy in first + second + third:
        copy.wait_send()


def reduced(packed, seqs, planes):
    rank, total = packed.shape
    group = seqs * CORES
    piece = total // group
    vmem = pl.BlockSpec(memory_space=pltpu.VMEM)
    dma = pltpu.SemaphoreType.DMA
    return pl.pallas_call(
        functools.partial(reduce_kernel, seqs, planes),
        in_specs=[vmem],
        out_specs=vmem,
        out_shape=jax.ShapeDtypeStruct((rank, total), BF16),
        scratch_shapes=[
            pltpu.VMEM((group - 1, rank, piece), BF16),
            pltpu.VMEM((planes, rank, piece), BF16),
            dma((group - 1,)),
            dma((group - 1,)),
            dma((max(planes - 1, 1),)),
            dma((max(planes - 1, 1),)),
            dma((group - 1,)),
            dma((group - 1,)),
        ],
        compiler_params=pltpu.CompilerParams(collective_id=0, has_side_effects=True),
        name="reduced",
    )(packed)


def shards(
    layer_input,
    frozen_queries,
    frozen_keys,
    frozen_values,
    output_gradient,
    norm_scale_vector,
    query_down_weight,
    query_up_weight,
    value_down_weight,
    value_up_weight,
    head_ordering,
):
    seqs = lax.axis_size("seq")
    planes = lax.axis_size("dp") // CORES
    rank, width = query_down_weight.shape
    queries = query_up_weight.shape[1]
    kv = value_up_weight.shape[1]
    half = head_ordering.shape[0] // 2
    odd = lax.axis_index("seq") % 2 == 1
    heads = jnp.where(odd, jnp.roll(head_ordering, -half), head_ordering)
    scale = norm_scale_vector.reshape(width // LANES, LANES)
    x, fq, grads, keys = layer_input[0], frozen_queries[0], output_gradient[0], frozen_keys[0]
    prior_keys = from_behind(keys, "seq", 1)
    inverse, qmid, vmid, values, given = prologue(
        heads, x, scale, query_down_weight, value_down_weight, frozen_values[0], value_up_weight, 4
    )
    prior_values = from_behind(given, "seq", 1)
    counts = ((half, half - 1), (0, half), (2 * half - 1, 1))
    attend = functools.partial(attention, heads=heads, fq=fq, grads=grads, keys=keys)
    attend = functools.partial(attend, values=values, mid=qmid, up=query_up_weight)
    dv_a, qb_a, dq_mid = attend(*counts[0], start=None, prior=None)
    dv_b, qb_b, dq_mid, dv_prior = attend(
        *counts[1], start=dq_mid, prior=(prior_keys, prior_values)
    )
    handed = from_behind(dv_prior, "seq", -1)
    dv_c, qb_c, dq_mid = attend(*counts[2], start=dq_mid, prior=None)
    used = 2 * width + queries + kv + width // rank
    unit = seqs * CORES * LANES
    total = -(-used // unit) * unit
    packed = epilogue(
        heads,
        counts,
        x,
        inverse,
        scale,
        query_down_weight,
        value_down_weight,
        dq_mid,
        handed,
        value_up_weight,
        vmid,
        (dv_a, dv_b, dv_c),
        (qb_a, qb_b, qb_c),
        total,
    )
    limit = math.sqrt(rank * (2 * width + queries + kv) + width)
    qa, gqb, va, vb, gain = finished(
        reduced(packed, seqs, planes), limit, (width, queries, width, kv), width
    )
    return (qa, gqb, va, vb, gain.reshape(width))


def solution(mesh):
    placed = (
        P("dp", "seq", None),
        P("dp", "seq", None),
        P("dp", "seq", None),
        P("dp", "seq", None),
        P("dp", "seq", None),
        P(),
        P(),
        P(),
        P(),
        P(),
        P(),
    )
    return jax.shard_map(
        shards, mesh=mesh, in_specs=placed, out_specs=(P(), P(), P(), P(), P()), check_vma=False
    )
```

```python
import functools
import math

import jax
import jax.numpy as jnp
from jax import lax
from jax.experimental import pallas as pl
from jax.experimental.pallas import tpu as pltpu
from jax.sharding import PartitionSpec as P

HEAD_SIZE = 128
CORES = 2
LANES = 128
TOGETHER = 8


EPS = 1e-05
ADAPTER_SCALE = 2.0
F32 = jnp.float32
BF16 = jnp.bfloat16
NT = (((1,), (1,)), ((), ()))
NN = (((1,), (0,)), ((), ()))


def from_behind(block, axis, distance):
    devices = range(lax.axis_size(axis))
    route = [((i - distance) % len(devices), i) for i in devices]
    return lax.ppermute(block, axis, route)


def dot(left, right, dims):
    return lax.dot_general(left, right, dims, preferred_element_type=F32)


def pick(order, slot):
    count = order.shape[0]
    shift = lax.rem(lax.axis_index("seq"), 2) * (count // 2)
    return order[lax.rem(slot + shift, count)]


def scaled(block, scale_ref, first, chunks):
    scale = scale_ref[pl.ds(first, chunks), :].astype(F32)
    return jnp.concatenate(
        [
            (block[:, i * LANES : (i + 1) * LANES] * scale[i : i + 1]).astype(BF16)
            for i in range(chunks)
        ],
        axis=1,
    )


def flipped(columns, start, count):
    rows = lax.broadcasted_iota(jnp.int32, (count, columns.shape[1]), 0)
    cols = lax.broadcasted_iota(jnp.int32, (count, columns.shape[1]), 1)
    pick = jnp.where(rows + start == cols, ADAPTER_SCALE, 0.0).astype(BF16)
    return dot(pick, columns, NT).astype(BF16)


def prologue_kernel(
    heads_ref,
    x_ref,
    scale_ref,
    qdown_ref,
    vdown_ref,
    fv_ref,
    vup_ref,
    inv_ref,
    qmid_ref,
    vmid_ref,
    value_ref,
    given_ref,
):
    width = x_ref.shape[1]
    hidden = x_ref[...].astype(F32)
    inverse = lax.rsqrt(jnp.sum(hidden * hidden, axis=-1, keepdims=True) * (1.0 / width) + EPS)
    inv_ref[...] = inverse
    normed = scaled(hidden * inverse, scale_ref, 0, width // LANES)
    qmid_ref[...] = dot(normed, qdown_ref[...], NT).astype(BF16)
    value_mid = dot(normed, vdown_ref[...], NT).astype(BF16)
    vmid_ref[...] = value_mid
    value_ref[...] = (
        fv_ref[...].astype(F32) + dot((value_mid * ADAPTER_SCALE).astype(BF16), vup_ref[...], NN)
    ).astype(BF16)
    half = given_ref.shape[1] // HEAD_SIZE
    for i in range(half):
        at = pl.multiple_of(pick(heads_ref, half + i) * HEAD_SIZE, HEAD_SIZE)
        given_ref[:, i * HEAD_SIZE : (i + 1) * HEAD_SIZE] = value_ref[:, pl.ds(at, HEAD_SIZE)]


def prologue(heads, x, scale, qdown, vdown, frozen_values, vup, steps):
    rows, width = x.shape
    block = rows // steps
    kv = frozen_values.shape[1]
    rank = qdown.shape[0]
    whole = lambda i, heads: (0, 0)
    by_rows = lambda i, heads: (i, 0)
    return pl.pallas_call(
        prologue_kernel,
        grid_spec=pltpu.PrefetchScalarGridSpec(
            num_scalar_prefetch=1,
            grid=(steps,),
            in_specs=[
                pl.BlockSpec((block, width), by_rows),
                pl.BlockSpec(scale.shape, whole),
                pl.BlockSpec(qdown.shape, whole),
                pl.BlockSpec(vdown.shape, whole),
                pl.BlockSpec((block, kv), by_rows),
                pl.BlockSpec(vup.shape, whole),
            ],
            out_specs=[
                pl.BlockSpec((block, 1), by_rows),
                pl.BlockSpec((block, rank), by_rows),
                pl.BlockSpec((block, rank), by_rows),
                pl.BlockSpec((block, kv), by_rows),
                pl.BlockSpec((block, kv // 2), by_rows),
            ],
        ),
        out_shape=[
            jax.ShapeDtypeStruct((rows, 1), F32),
            jax.ShapeDtypeStruct((rows, rank), BF16),
            jax.ShapeDtypeStruct((rows, rank), BF16),
            jax.ShapeDtypeStruct((rows, kv), BF16),
            jax.ShapeDtypeStruct((rows, kv // 2), BF16),
        ],
        cost_estimate=pl.CostEstimate(
            flops=40 * rows * width, bytes_accessed=2 * rows * width, transcendentals=0
        ),
        name="prologue",
    )(heads, x, scale, qdown, vdown, frozen_values, vup)


def attention_kernel(has_start, with_prior, heads_ref, *refs):
    refs = list(refs)
    fq_ref, grad_ref, key_ref, value_ref, mid_ref, up_ref = refs[:6]
    refs = refs[6:]
    if has_start:
        start_ref = refs.pop(0)
    if with_prior:
        prior_key_ref, prior_value_ref = refs.pop(0), refs.pop(0)
    dv_ref, qb_ref, dq_mid_ref = refs[:3]
    rows = fq_ref.shape[0]
    heads = fq_ref.shape[1] // HEAD_SIZE
    rank = up_ref.shape[0]
    factor = 1.0 / math.sqrt(HEAD_SIZE)

    @pl.when(pl.program_id(0) == 0)
    def _():
        dq_mid_ref[...] = start_ref[...] if has_start else jnp.zeros_like(dq_mid_ref)

    keys = key_ref[...]
    values = value_ref[...]
    if with_prior:
        keys = jnp.concatenate([keys, prior_key_ref[...]], axis=0)
        values = jnp.concatenate([values, prior_value_ref[...]], axis=0)
    keys_t = keys.T
    query_mid = (mid_ref[...] * ADAPTER_SCALE).astype(BF16)
    mid_t = flipped(mid_ref[...], 0, rank)
    key_pos = lax.broadcasted_iota(jnp.int32, (rows, rows), 0)
    query_pos = lax.broadcasted_iota(jnp.int32, (rows, rows), 1)
    causal = key_pos <= query_pos
    together = math.gcd(heads, TOGETHER)
    up = up_ref[...]
    query = (fq_ref[...].astype(F32) + dot(query_mid, up, NN)).astype(BF16)
    dv = None
    dqueries = []
    for j in range(0, heads, together):
        stacked = lambda array: jnp.concatenate(
            [array[:, i * HEAD_SIZE : (i + 1) * HEAD_SIZE] for i in range(j, j + together)], axis=0
        )
        grad = stacked(grad_ref)
        scores = dot(keys, stacked(query), NT)
        own = jnp.concatenate(
            [
                jnp.where(causal, scores[:rows, i * rows : (i + 1) * rows], -jnp.inf)
                for i in range(together)
            ],
            axis=1,
        )
        scores = jnp.concatenate([own, scores[rows:]], axis=0) if with_prior else own
        top = jnp.max(scores, axis=0, keepdims=True)
        exponent = jnp.exp2((scores - top) * (factor * math.log2(math.e)))
        probs = exponent * (1.0 / jnp.sum(exponent, axis=0, keepdims=True))
        weights = probs.astype(BF16)
        dprob = dot(values, grad, NT)
        delta = jnp.sum(weights.astype(F32) * dprob, axis=0, keepdims=True)
        dscore = (probs * (dprob - delta)).astype(BF16)
        term = dot(weights, grad, NN)
        dv = term if dv is None else dv + term
        dquery = (dot(keys_t, dscore, NN) * factor).astype(BF16)
        dqueries += [dquery[:, i * rows : (i + 1) * rows] for i in range(together)]
    dquery = jnp.concatenate(dqueries, axis=0)
    qb_ref[...] = dot(mid_t, dquery, NT)
    dq_mid_ref[...] += dot(up, dquery, NN)
    dv_ref[...] = dv[:rows]
    if with_prior:
        refs[3][...] = dv[rows:].astype(BF16)


def attention(first, count, heads, fq, grads, keys, values, mid, up, start, prior):
    rows, queries = fq.shape
    kv_heads = keys.shape[1] // HEAD_SIZE
    wide = queries // kv_heads
    rank = up.shape[0]
    by_head = lambda i, heads: (0, pick(heads, first + i))
    by_slot = lambda i, heads: (0, i)
    whole = lambda i, heads: (0, 0)
    narrow = pl.BlockSpec((rows, HEAD_SIZE), by_head)
    broad = pl.BlockSpec((rows, wide), by_head)
    slot = pl.BlockSpec((rows, HEAD_SIZE), by_slot)
    operands = [fq, grads, keys, values, mid, up]
    in_specs = [
        broad,
        broad,
        narrow,
        narrow,
        pl.BlockSpec(mid.shape, whole),
        pl.BlockSpec((rank, wide), by_head),
    ]
    out_specs = [
        slot,
        pl.BlockSpec((rank, wide), by_slot),
        pl.BlockSpec((rank, rows), whole),
    ]
    out_shape = [
        jax.ShapeDtypeStruct((rows, count * HEAD_SIZE), F32),
        jax.ShapeDtypeStruct((rank, count * wide), F32),
        jax.ShapeDtypeStruct((rank, rows), F32),
    ]
    if start is not None:
        operands.append(start)
        in_specs.append(pl.BlockSpec(start.shape, whole))
    if prior is not None:
        operands += list(prior)
        in_specs += [narrow, slot]
        out_specs.append(slot)
        out_shape.append(jax.ShapeDtypeStruct((rows, count * HEAD_SIZE), BF16))
    return pl.pallas_call(
        functools.partial(attention_kernel, start is not None, prior is not None),
        grid_spec=pltpu.PrefetchScalarGridSpec(
            num_scalar_prefetch=1, grid=(count,), in_specs=in_specs, out_specs=out_specs
        ),
        out_shape=out_shape,
        cost_estimate=pl.CostEstimate(
            flops=count * 24 * rows * rows * wide,
            bytes_accessed=count * 4 * rows * wide,
            transcendentals=0,
        ),
        name="attention",
    )(heads, *operands)


def epilogue_kernel(
    counts,
    heads_ref,
    x_ref,
    inv_ref,
    scale_ref,
    qdown_ref,
    vdown_ref,
    dq_mid_ref,
    handed_ref,
    vup_ref,
    vmid_ref,
    *refs,
):
    dv_refs, qb_refs = refs[: len(counts)], refs[len(counts) : 2 * len(counts)]
    packed_ref, inner_ref, gain_ref = refs[2 * len(counts) :]
    step = pl.program_id(0)
    block = x_ref.shape[1]
    rank = vup_ref.shape[0]
    full = gain_ref.shape[0] * block
    kv = vup_ref.shape[1]
    half = handed_ref.shape[1] // HEAD_SIZE
    wide = qb_refs[0].shape[1] // counts[0][1]
    queries = kv // HEAD_SIZE * wide
    base = 2 * full + queries

    @pl.when(step == 0)
    def _():
        mid_t = flipped(vmid_ref[...], 0, rank)
        dv_mid = jnp.zeros(dq_mid_ref.shape, F32)
        for (first, count), dv_ref, qb_ref in zip(counts, dv_refs, qb_refs):
            for i in range(count):
                cols = slice(i * HEAD_SIZE, (i + 1) * HEAD_SIZE)
                dv = dv_ref[:, cols]
                if first + i >= half:
                    given = first + i - half
                    other = handed_ref[:, given * HEAD_SIZE : (given + 1) * HEAD_SIZE]
                    dv = dv + other.astype(F32)
                dv = dv.astype(BF16)
                head = pick(heads_ref, first + i)
                at = pl.multiple_of(head * HEAD_SIZE, HEAD_SIZE)
                dv_mid = dv_mid + dot(vup_ref[:, pl.ds(at, HEAD_SIZE)], dv, NT)
                at = pl.multiple_of(base + head * HEAD_SIZE, HEAD_SIZE)
                packed_ref[:, pl.ds(at, HEAD_SIZE)] = dot(mid_t, dv, NN).astype(BF16)
                at = pl.multiple_of(2 * full + head * wide, HEAD_SIZE)
                packed_ref[:, pl.ds(at, wide)] = qb_ref[:, i * wide : (i + 1) * wide].astype(BF16)
        inner_ref[...] = (
            ADAPTER_SCALE * jnp.concatenate([dq_mid_ref[...], dv_mid], axis=0)
        ).astype(BF16)
        gain_ref[...] = jnp.zeros_like(gain_ref)
        used = base + kv + block
        if used < packed_ref.shape[1]:
            packed_ref[:, used:] = jnp.zeros((rank, packed_ref.shape[1] - used), BF16)

    inner = inner_ref[...]
    unit = x_ref[...].astype(F32) * inv_ref[...]
    normed = scaled(unit, scale_ref, 0, block // LANES)
    raw = dot(inner, normed, NN).astype(BF16)
    at = pl.multiple_of(step * block, block)
    packed_ref[:, pl.ds(at, block)] = raw[:rank]
    packed_ref[:, pl.ds(at + full, block)] = raw[rank:]
    spread = dot(inner, unit.astype(BF16), NN)
    gain = jnp.sum(
        qdown_ref[...].astype(F32) * spread[:rank] + vdown_ref[...].astype(F32) * spread[rank:],
        axis=0,
        keepdims=True,
    )
    row = lax.broadcasted_iota(jnp.int32, gain_ref.shape, 0)
    gain_ref[...] = jnp.where(row == step, gain, gain_ref[...])

    @pl.when(step == pl.num_programs(0) - 1)
    def _():
        packed_ref[:, base + kv : base + kv + block] = gain_ref[...].astype(BF16)


def epilogue(heads, counts, x, inverse, scale, qdown, vdown, dq_mid, handed, vup, vmid, dvs, qbs, total):
    rows, width = x.shape
    rank = vup.shape[0]
    block = width // rank
    whole = lambda j, heads: (0, 0)
    by_cols = lambda j, heads: (0, j)
    kept = lambda a: pl.BlockSpec(a.shape, whole)
    return pl.pallas_call(
        functools.partial(epilogue_kernel, counts),
        grid_spec=pltpu.PrefetchScalarGridSpec(
            num_scalar_prefetch=1,
            grid=(rank,),
            in_specs=[
                pl.BlockSpec((rows, block), by_cols),
                kept(inverse),
                pl.BlockSpec((block // LANES, LANES), lambda j, heads: (j, 0)),
                pl.BlockSpec((rank, block), by_cols),
                pl.BlockSpec((rank, block), by_cols),
                kept(dq_mid),
                kept(handed),
                kept(vup),
                kept(vmid),
            ]
            + [kept(a) for a in (*dvs, *qbs)],
            out_specs=pl.BlockSpec((rank, total), whole),
            scratch_shapes=[
                pltpu.VMEM((2 * rank, rows), BF16),
                pltpu.VMEM((rank, block), F32),
            ],
        ),
        out_shape=jax.ShapeDtypeStruct((rank, total), BF16),
        cost_estimate=pl.CostEstimate(
            flops=80 * rows * width, bytes_accessed=2 * rows * width, transcendentals=0
        ),
        name="epilogue",
    )(heads, x, inverse, scale, qdown, vdown, dq_mid, handed, vup, vmid, *dvs, *qbs)


def finish_kernel(limit, full_ref, qa_ref, qb_ref, va_ref, vb_ref, gain_ref):
    sums = full_ref[...].astype(F32)
    squares = jnp.sum(jnp.sum(sums * sums, axis=1, keepdims=True), axis=0, keepdims=True)
    scale = jnp.minimum(1.0, limit / jnp.sqrt(squares))
    at = 0
    for out in (qa_ref, va_ref, qb_ref, vb_ref):
        out[...] = full_ref[:, at : at + out.shape[1]].astype(F32) * scale
        at += out.shape[1]
    rank = full_ref.shape[0]
    chunks = gain_ref.shape[0] // rank
    for c in range(chunks):
        piece = full_ref[:, at + c * LANES : at + (c + 1) * LANES].astype(F32) * scale
        gain_ref[pl.ds(c, rank, stride=chunks), :] = piece


def finished(full, limit, widths, width):
    rank = full.shape[0]
    vmem = pl.BlockSpec(memory_space=pltpu.VMEM)
    return pl.pallas_call(
        functools.partial(finish_kernel, limit),
        in_specs=[vmem],
        out_specs=[vmem] * (len(widths) + 1),
        out_shape=[jax.ShapeDtypeStruct((rank, w), F32) for w in widths]
        + [jax.ShapeDtypeStruct((width // LANES, LANES), F32)],
        name="finished",
    )(full)


def reduce_kernel(
    seqs,
    planes,
    packed_ref,
    full,
    parts,
    column,
    send_one,
    recv_one,
    send_two,
    recv_two,
    send_three,
    recv_three,
):
    group = seqs * CORES
    piece = full.shape[1] // group
    place = lax.axis_index("dp")
    plane = place // CORES
    me = lax.axis_index("seq") * CORES + place % CORES

    def in_group(k):
        peer = lax.rem(me + k, group)
        return peer, {"seq": peer // CORES, "dp": plane * CORES + peer % CORES}

    def in_column(k):
        return {"dp": lax.rem(plane + k, planes) * CORES + place % CORES}

    def span(index):
        return pl.ds(pl.multiple_of(index * piece, piece), piece)

    barrier = pltpu.get_barrier_semaphore()
    for k in range(1, group):
        pl.semaphore_signal(
            barrier, inc=1, device_id=in_group(k)[1], device_id_type=pl.DeviceIdType.MESH
        )
    for k in range(1, planes):
        pl.semaphore_signal(
            barrier, inc=1, device_id=in_column(k), device_id_type=pl.DeviceIdType.MESH
        )
    pl.semaphore_wait(barrier, group + planes - 2)

    def remote(source, target, send, recv, device):
        copy = pltpu.make_async_remote_copy(
            src_ref=source,
            dst_ref=target,
            send_sem=send,
            recv_sem=recv,
            device_id=device,
            device_id_type=pl.DeviceIdType.MESH,
        )
        copy.start()
        return copy

    first = []
    for k in range(1, group):
        peer, device = in_group(k)
        first.append(
            remote(
                packed_ref.at[:, span(peer)],
                parts.at[k - 1],
                send_one.at[k - 1],
                recv_one.at[k - 1],
                device,
            )
        )
    total = packed_ref[:, span(me)].astype(F32)
    for k in range(1, group):
        first[k - 1].wait_recv()
        total = total + parts[k - 1].astype(F32)
    column[plane] = total.astype(BF16)
    second = [
        remote(
            column.at[plane],
            column.at[plane],
            send_two.at[k - 1],
            recv_two.at[k - 1],
            in_column(k),
        )
        for k in range(1, planes)
    ]
    for copy in second:
        copy.wait_recv()
    total = column[0].astype(F32)
    for i in range(1, planes):
        total = total + column[i].astype(F32)
    full[:, span(me)] = total.astype(BF16)
    third = [
        remote(
            full.at[:, span(me)],
            full.at[:, span(me)],
            send_three.at[k - 1],
            recv_three.at[k - 1],
            in_group(k)[1],
        )
        for k in range(1, group)
    ]
    for copy in third:
        copy.wait_recv()
    for copy in first + second + third:
        copy.wait_send()


def reduced(packed, seqs, planes):
    rank, total = packed.shape
    group = seqs * CORES
    piece = total // group
    vmem = pl.BlockSpec(memory_space=pltpu.VMEM)
    dma = pltpu.SemaphoreType.DMA
    return pl.pallas_call(
        functools.partial(reduce_kernel, seqs, planes),
        in_specs=[vmem],
        out_specs=vmem,
        out_shape=jax.ShapeDtypeStruct((rank, total), BF16),
        scratch_shapes=[
            pltpu.VMEM((group - 1, rank, piece), BF16),
            pltpu.VMEM((planes, rank, piece), BF16),
            dma((group - 1,)),
            dma((group - 1,)),
            dma((max(planes - 1, 1),)),
            dma((max(planes - 1, 1),)),
            dma((group - 1,)),
            dma((group - 1,)),
        ],
        compiler_params=pltpu.CompilerParams(collective_id=0, has_side_effects=True),
        name="reduced",
    )(packed)


def shards(
    layer_input,
    frozen_queries,
    frozen_keys,
    frozen_values,
    output_gradient,
    norm_scale_vector,
    query_down_weight,
    query_up_weight,
    value_down_weight,
    value_up_weight,
    head_ordering,
):
    seqs = lax.axis_size("seq")
    planes = lax.axis_size("dp") // CORES
    rank, width = query_down_weight.shape
    queries = query_up_weight.shape[1]
    kv = value_up_weight.shape[1]
    half = head_ordering.shape[0] // 2
    heads = head_ordering
    scale = norm_scale_vector.reshape(width // LANES, LANES)
    x, fq, grads, keys = layer_input[0], frozen_queries[0], output_gradient[0], frozen_keys[0]
    prior_keys = from_behind(keys, "seq", 1)
    inverse, qmid, vmid, values, given = prologue(
        heads, x, scale, query_down_weight, value_down_weight, frozen_values[0], value_up_weight, 4
    )
    prior_values = from_behind(given, "seq", 1)
    counts = ((half, half - 1), (0, half), (2 * half - 1, 1))
    attend = functools.partial(attention, heads=heads, fq=fq, grads=grads, keys=keys)
    attend = functools.partial(attend, values=values, mid=qmid, up=query_up_weight)
    dv_a, qb_a, dq_mid = attend(*counts[0], start=None, prior=None)
    dv_b, qb_b, dq_mid, dv_prior = attend(
        *counts[1], start=dq_mid, prior=(prior_keys, prior_values)
    )
    handed = from_behind(dv_prior, "seq", -1)
    dv_c, qb_c, dq_mid = attend(*counts[2], start=dq_mid, prior=None)
    used = 2 * width + queries + kv + width // rank
    unit = seqs * CORES * LANES
    total = -(-used // unit) * unit
    packed = epilogue(
        heads,
        counts,
        x,
        inverse,
        scale,
        query_down_weight,
        value_down_weight,
        dq_mid,
        handed,
        value_up_weight,
        vmid,
        (dv_a, dv_b, dv_c),
        (qb_a, qb_b, qb_c),
        total,
    )
    limit = math.sqrt(rank * (2 * width + queries + kv) + width)
    qa, gqb, va, vb, gain = finished(
        reduced(packed, seqs, planes), limit, (width, queries, width, kv), width
    )
    return (qa, gqb, va, vb, gain.reshape(width))


def solution(mesh):
    placed = (
        P("dp", "seq", None),
        P("dp", "seq", None),
        P("dp", "seq", None),
        P("dp", "seq", None),
        P("dp", "seq", None),
        P(),
        P(),
        P(),
        P(),
        P(),
        P(),
    )
    return jax.shard_map(
        shards, mesh=mesh, in_specs=placed, out_specs=(P(), P(), P(), P(), P()), check_vma=False
    )
```
